128 devices in a mesh: rows: 32 (over x_hi, z, y), layers: 4 (over x_lo, core).
Axes of the slice: x: 4 (x_hi: 2, x_lo: 2; x = x_hi * 2 + x_lo), y: 4, z: 4, core: 2. Of those that a mesh axis runs over, the one named last changes fastest.
Arguments:
- queries: bfloat16 [1024, 4, 4096], P('rows', 'layers'), may hold values from -6 to 6
- precond: bfloat16 [4, 4096, 4096], P('layers', None, 'rows'), as said below
- train_grads: bfloat16 [65536, 4, 4096], P('rows', 'layers'), may hold values from -0.09375 to 0.09375
Outputs:
- scores: float32 [1024, 65536], P('layers', 'rows')
The draws below stay inside these ranges and needn't reach their ends.
Inputs may be any that keep to these rules, and one draw needn't show every extreme that they name: `precond`: symmetric in its last two dimensions.
All inputs are finite; a program needn't handle non-finite values.
Results may differ from the reference program's by a relative error of at most 0.0029.
Values may be sent and summed in bfloat16 or wider, within the bound.
No kernel may reach another device: no remote copies, remote signals or barrier semaphores. Data moves between devices by JAX's collectives and lax.ppermute only.
A program may use at most 128 MiB of HBM per device.

```python
import jax
import jax.numpy as jnp

F = 4096
LAYERS = 4
NQ = 1024
NT = 65536


def draw_precond(key, part):
    key_off = jax.random.fold_in(key, 11)
    key_diag = jax.random.fold_in(key, 12)
    noise = jax.random.normal(key_off, (LAYERS, F, F), jnp.float32) * (0.5 / F ** 0.5)
    sym = noise + jnp.swapaxes(noise, 1, 2)
    diag_vals = jax.random.uniform(key_diag, (LAYERS, F), jnp.float32, 0.5, 2.0)
    eye_mask = (jnp.arange(F)[:, None] == jnp.arange(F)[None, :]).astype(jnp.float32)
    matrix = sym + eye_mask[None, :, :] * diag_vals[:, :, None]
    return matrix.astype(jnp.bfloat16)


def levels(key, dims, shards, least, top_value):
    def one(position, blocks):
        draws = jax.random.uniform(jax.random.fold_in(jax.random.fold_in(key, 6), position), (blocks,), jnp.float32, least / len(shards), top_value / len(shards))
        return jnp.repeat(jnp.exp(draws), dims[position] // blocks).reshape((-1,) + (1,) * (len(dims) - position - 1))

    level = one(*shards[0])
    for cut in shards[1:]:
        level = level * one(*cut)
    return level


def bell_draw(stream_key, extent, width, reach, split=(), kind=jnp.bfloat16):
    gain = levels(stream_key, extent, split, -0.22, 0.18) if split else 1.0
    array = jax.random.normal(stream_key, extent, jnp.float32) * width * gain
    return jnp.minimum(jnp.maximum(array, -reach), reach).astype(kind)


def setup_inputs(seed: int = 0) -> dict:
    key_of = jax.random.split(jax.random.key(seed), 4)
    queries = bell_draw(key_of[0], (NQ, LAYERS, F), 1.0, 6.0, ((0, 32), (1, 4)))
    precond = draw_precond(jax.random.fold_in(key_of[3], 71), 0)
    train_grads = bell_draw(key_of[2], (NT, LAYERS, F), F ** -0.5, 0.09375, ((0, 32), (1, 4)))
    return {"queries": queries, "precond": precond, "train_grads": train_grads}


def reference(queries, precond, train_grads):
    scores = jnp.zeros((NQ, NT), jnp.float32)
    for layer in range(LAYERS):
        conditioned = jnp.dot(queries[:, layer, :], precond[layer], preferred_element_type=jnp.float32).astype(jnp.bfloat16)
        scores = scores + jnp.dot(conditioned, train_grads[:, layer, :].T, preferred_element_type=jnp.float32)
    return scores
```

```python
import functools

import jax
import jax.numpy as jnp
from jax import lax
from jax.experimental import pallas as pl
from jax.experimental.pallas import tpu as pltpu
from jax.sharding import PartitionSpec as P

F = 4096
COLS = 128
SUB = 16
RA = 16 * SUB
TT = 512
NTL = 2048
TILES = (((0, 4),), ((0, 3), (3, 1)))


def perm_of(f):
    pairs = []
    for r in range(32):
        xh, z, y = r // 16, (r // 4) % 4, r % 4
        a, b, c = f(xh, z, y)
        pairs.append((r, (a % 2) * 16 + (b % 4) * 4 + c % 4))
    return pairs


UP_Y = perm_of(lambda a, b, c: (a, b, c + 1))
DOWN_Y = perm_of(lambda a, b, c: (a, b, c - 1))
UP_Z = perm_of(lambda a, b, c: (a, b + 1, c))
DOWN_Z = perm_of(lambda a, b, c: (a, b - 1, c))
CORNER = perm_of(lambda a, b, c: (a, b + 2, c + 2))
XH = perm_of(lambda a, b, c: (a + 1, b, c))
CORE = [(0, 1), (1, 0), (2, 3), (3, 2)]
XL = [(0, 2), (2, 0), (1, 3), (3, 1)]


def send4(to_up_y, to_down_y, to_up_z, to_down_z):
    return [
        lax.ppermute(x, "rows", perm)
        for x, perm in ((to_up_y, UP_Y), (to_down_y, DOWN_Y), (to_up_z, UP_Z), (to_down_z, DOWN_Z))
    ]


NEAR = ((0, 0), (0, 3), (0, 1), (3, 0), (1, 0))
DIAGONAL = ((3, 3), (1, 1), (3, 1), (1, 3))
FAR = ((0, 2), (0, 2), (2, 0), (2, 0))
KNIGHT = ((3, 2), (1, 2), (2, 1), (2, 3))


def flood(block):
    near = [block] + send4(block, block, block, block)
    _, ly, ry, lz, rz = near
    cat = lambda a, b: jnp.concatenate([a, b], axis=0)
    two = send4(cat(lz, ly[:1]), cat(rz, ry[1:]), cat(ry, lz[:1]), cat(ly, rz[1:]))
    three = send4(*[x[:2] for x in two])
    return [*near, *two, *three, lax.ppermute(block, "rows", CORNER)]


def condition_kernel(pos, *refs):
    near, two, three, (corner, own, other, out, q, p, sem) = refs[:5], refs[5:9], refs[9:13], refs[13:]
    xh, z, y = pos[0], pos[1], pos[2]
    at = lambda d: ((z + d[0]) % 4) * 4 + (y + d[1]) % 4
    copies = [(own, p.at[:, pl.ds(pl.multiple_of(xh * COLS, COLS), COLS)])]
    copies += [(other, p.at[:, pl.ds(pl.multiple_of((1 - xh) * COLS, COLS), COLS)])]
    copies += [(x, q.at[at(d)]) for x, d in zip(near, NEAR)]
    copies += [(x.at[0:2], q.at[at(d)]) for x, d in zip(two, DIAGONAL)]
    copies += [(x.at[2], q.at[at(d), k % 2]) for k, (x, d) in enumerate(zip(two, FAR))]
    copies += [(x, q.at[at(d)]) for x, d in zip(three, KNIGHT)]
    copies += [(corner, q.at[at((2, 2))])]
    copies = [pltpu.make_async_copy(src, dst, sem.at[i]) for i, (src, dst) in enumerate(copies)]
    for c in copies:
        c.start()
    for c in copies:
        c.wait()
    s = jnp.dot(q[...].reshape(2 * RA, F), p[...], preferred_element_type=jnp.float32)
    s = s.astype(jnp.bfloat16).reshape(16, 2, SUB, 2 * COLS)
    for chunk in range(2):
        for h in range(2):
            out[chunk, h] = s[:, chunk, :, h * COLS : (h + 1) * COLS].reshape(RA, COLS)


def condition(pos, pieces, own, other):
    return pl.pallas_call(
        condition_kernel,
        out_shape=jax.ShapeDtypeStruct((2, 2, RA, COLS), jnp.bfloat16),
        in_specs=[pl.BlockSpec(memory_space=pltpu.SMEM)] + [pl.BlockSpec(memory_space=pltpu.HBM)] * 16,
        out_specs=pl.BlockSpec(memory_space=pltpu.VMEM),
        scratch_shapes=[
            pltpu.VMEM((16, 2, SUB, F), jnp.bfloat16),
            pltpu.VMEM((F, 2 * COLS), jnp.bfloat16),
            pltpu.SemaphoreType.DMA((20,)),
        ],
        compiler_params=pltpu.CompilerParams(vmem_limit_bytes=24 << 20),
        cost_estimate=pl.CostEstimate(flops=4 * RA * F * 256, bytes_accessed=6 << 20, transcendentals=0),
        name="condition",
    )(pos, *pieces, own, other)


def score_kernel(chunk, pos, *refs):
    near, two, three, (corner, t, keep, send, c, sem) = refs[:5], refs[5:9], refs[9:13], refs[13:]
    xh, z, y, xl, core = (pos[i] for i in range(5))

    @pl.when(pl.program_id(0) == 0)
    def _():
        at = lambda d: c.at[:, :, :, pl.ds(pl.multiple_of((((z + d[0]) % 4) * 4 + (y + d[1]) % 4) * COLS, COLS), COLS)]
        copies = [(x.at[chunk], at(d)) for x, d in zip(near, NEAR)]
        copies += [(x.at[chunk], at(d)) for x, d in zip(two, DIAGONAL)]
        copies += [(two[k].at[2], at(FAR[k])) for k in (chunk, 2 + chunk)]
        copies += [(x.at[chunk], at(d)) for x, d in zip(three, KNIGHT)]
        copies += [(corner.at[chunk], at((2, 2)))]
        copies = [pltpu.make_async_copy(src, dst, sem.at[i]) for i, (src, dst) in enumerate(copies)]
        for x in copies:
            x.start()
        for x in copies:
            x.wait()

    s = 0.0
    for h in range(2):
        s += lax.dot_general(
            c[:, h].reshape(2 * RA, F // 2),
            t[:, h * (F // 2) : (h + 1) * (F // 2)],
            (((1,), (1,)), ((), ())),
            preferred_element_type=jnp.float32,
        )
    s = s.reshape(2, 2, RA // 2, TT)
    same = xh == xl
    for i in range(2):
        own = jnp.where(same, s[i], s[1 - i])
        keep[i] = jnp.where(core == 0, own[0], own[1])
        send[i] = jnp.where(core == 0, own[1], own[0]).astype(jnp.bfloat16)


def score(pos, pieces, train, chunk, first, steps):
    return pl.pallas_call(
        functools.partial(score_kernel, chunk),
        grid=(steps,),
        out_shape=(
            jax.ShapeDtypeStruct((2, RA // 2, steps * TT), jnp.float32),
            jax.ShapeDtypeStruct((2, RA // 2, steps * TT), jnp.bfloat16),
        ),
        in_specs=[pl.BlockSpec(memory_space=pltpu.SMEM)]
        + [pl.BlockSpec(memory_space=pltpu.HBM)] * 14
        + [pl.BlockSpec((TT, F), lambda i: (i + first, 0))],
        out_specs=(
            pl.BlockSpec((2, RA // 2, TT), lambda i: (0, 0, i)),
            pl.BlockSpec((2, RA // 2, TT), lambda i: (0, 0, i)),
        ),
        scratch_shapes=[pltpu.VMEM((2, 2, RA, F // 2), jnp.bfloat16), pltpu.SemaphoreType.DMA((16,))],
        compiler_params=pltpu.CompilerParams(vmem_limit_bytes=36 << 20),
        cost_estimate=pl.CostEstimate(
            flops=2 * 2 * RA * F * steps * TT, bytes_accessed=(RA * F * 4 + steps * TT * F * 2), transcendentals=0
        ),
        name="score",
    )(pos, *pieces, train)


def per_device(queries, precond, train_grads):
    r, l = lax.axis_index("rows"), lax.axis_index("layers")
    pos = jnp.stack([r // 16, (r // 4) % 4, r % 4, l // 2, l % 2]).astype(jnp.int32)
    q = queries.reshape(2, SUB, F)
    p = precond.reshape(F, COLS)
    train = pltpu.with_memory_space_constraint(train_grads.reshape(NTL, F), pltpu.HBM)
    p_other = lax.ppermute(p, "rows", XH)

    cond = condition(pos, flood(q), p, p_other)

    partner = lax.ppermute(cond, "rows", XH)
    pieces = flood(jnp.stack([cond, partner], axis=1))
    out = jnp.zeros((8, 2, SUB, NTL), jnp.float32)
    for chunk in range(2):
        for first, steps in TILES[chunk]:
            keep, send = score(pos, pieces, train, chunk, first, steps)
            got = lax.ppermute(send, "layers", CORE)
            away = (keep[1] + got[1].astype(jnp.float32)).astype(jnp.bfloat16)
            if chunk == 0:
                pos, away = lax.optimization_barrier((pos, away))
            back = lax.ppermute(away, "layers", XL)
            total = keep[0] + got[0].astype(jnp.float32) + back.astype(jnp.float32)
            out = lax.dynamic_update_slice(out, total.reshape(8, 1, SUB, steps * TT), (0, chunk, 0, first * TT))
            if chunk == 0:
                pos_late, out = lax.optimization_barrier((pos, out))
            elif first == 0:
                pos = pos_late
    return out.reshape(256, NTL)


def solution(mesh):
    return jax.shard_map(
        per_device,
        mesh=mesh,
        in_specs=(P("rows", "layers", None), P("layers", None, "rows"), P("rows", "layers", None)),
        out_specs=P("layers", "rows"),
        check_vma=False,
    )
```

```python
import functools

import jax
import jax.numpy as jnp
from jax import lax
from jax.experimental import pallas as pl
from jax.experimental.pallas import tpu as pltpu
from jax.sharding import PartitionSpec as P

F = 4096
COLS = 128
SUB = 16
RA = 16 * SUB
TT = 512
NTL = 2048


def perm_of(f):
    pairs = []
    for r in range(32):
        xh, z, y = r // 16, (r // 4) % 4, r % 4
        a, b, c = f(xh, z, y)
        pairs.append((r, (a % 2) * 16 + (b % 4) * 4 + c % 4))
    return pairs


UP_Y = perm_of(lambda a, b, c: (a, b, c + 1))
DOWN_Y = perm_of(lambda a, b, c: (a, b, c - 1))
UP_Z = perm_of(lambda a, b, c: (a, b + 1, c))
DOWN_Z = perm_of(lambda a, b, c: (a, b - 1, c))
FAR_Y = perm_of(lambda a, b, c: (a, b, c + 2))
FAR_Z = perm_of(lambda a, b, c: (a, b + 2, c))
XH = perm_of(lambda a, b, c: (a + 1, b, c))
CORE = [(0, 1), (1, 0), (2, 3), (3, 2)]
XL = [(0, 2), (2, 0), (1, 3), (3, 1)]


def send4(to_up_y, to_down_y, to_up_z, to_down_z):
    return [
        lax.ppermute(x, "rows", perm)
        for x, perm in ((to_up_y, UP_Y), (to_down_y, DOWN_Y), (to_up_z, UP_Z), (to_down_z, DOWN_Z))
    ]


NEAR = ((0, 0), (0, 3), (0, 1), (3, 0), (1, 0))
DIAGONAL = ((3, 3), (1, 1), (3, 1), (1, 3))
FAR = ((0, 2), (0, 2), (2, 0), (2, 0))
KNIGHT = ((3, 2), (1, 2), (2, 1), (2, 3))


def flood(block):
    near = [block] + send4(block, block, block, block)
    _, ly, ry, lz, rz = near
    cat = lambda a, b: jnp.concatenate([a, b], axis=0)
    two = send4(cat(lz, ly[:1]), cat(rz, ry[1:]), cat(ry, lz[:1]), cat(ly, rz[1:]))
    corner0 = lax.ppermute(two[2][2], "rows", FAR_Y)
    three = send4(*[x[:2] for x in two])
    corner1 = lax.ppermute(two[1][2], "rows", FAR_Z)
    return [*near, *two, *three, corner0, corner1]


def condition_kernel(pos, *refs):
    near, two, three, corner = refs[:5], refs[5:9], refs[9:13], refs[13:15]
    own, other, out, q, p, sem = refs[15:]
    xh, z, y = pos[0], pos[1], pos[2]
    at = lambda d: ((z + d[0]) % 4) * 4 + (y + d[1]) % 4
    copies = [(own, p.at[:, pl.ds(pl.multiple_of(xh * COLS, COLS), COLS)])]
    copies += [(other, p.at[:, pl.ds(pl.multiple_of((1 - xh) * COLS, COLS), COLS)])]
    copies += [(x, q.at[at(d)]) for x, d in zip(near, NEAR)]
    copies += [(x.at[0:2], q.at[at(d)]) for x, d in zip(two, DIAGONAL)]
    copies += [(x.at[2], q.at[at(d), k % 2]) for k, (x, d) in enumerate(zip(two, FAR))]
    copies += [(x, q.at[at(d)]) for x, d in zip(three, KNIGHT)]
    copies += [(x, q.at[at((2, 2)), k]) for k, x in enumerate(corner)]
    copies = [pltpu.make_async_copy(src, dst, sem.at[i]) for i, (src, dst) in enumerate(copies)]
    for c in copies:
        c.start()
    for c in copies:
        c.wait()
    s = jnp.dot(q[...].reshape(2 * RA, F), p[...], preferred_element_type=jnp.float32)
    s = s.astype(jnp.bfloat16).reshape(16, 2, SUB, 2 * COLS)
    for chunk in range(2):
        for h in range(2):
            out[chunk, h] = s[:, chunk, :, h * COLS : (h + 1) * COLS].reshape(RA, COLS)


def condition(pos, pieces, own, other):
    return pl.pallas_call(
        condition_kernel,
        out_shape=jax.ShapeDtypeStruct((2, 2, RA, COLS), jnp.bfloat16),
        in_specs=[pl.BlockSpec(memory_space=pltpu.SMEM)]
        + [pl.BlockSpec(memory_space=pltpu.HBM)] * 15
        + [pl.BlockSpec(memory_space=pl.ANY)] * 2,
        out_specs=pl.BlockSpec(memory_space=pltpu.VMEM),
        scratch_shapes=[
            pltpu.VMEM((16, 2, SUB, F), jnp.bfloat16),
            pltpu.VMEM((F, 2 * COLS), jnp.bfloat16),
            pltpu.SemaphoreType.DMA((21,)),
        ],
        compiler_params=pltpu.CompilerParams(vmem_limit_bytes=24 << 20),
        cost_estimate=pl.CostEstimate(flops=4 * RA * F * 256, bytes_accessed=6 << 20, transcendentals=0),
        name="condition",
    )(pos, *pieces, own, other)


def split(s, same, core, keep, send):
    for i in range(2):
        own = jnp.where(same, s[i], s[1 - i])
        keep[i] = jnp.where(core == 0, own[0], own[1])
        send[i] = jnp.where(core == 0, own[1], own[0]).astype(jnp.bfloat16)


def near_blocks(chunk):
    return [(k, chunk, d) for k, d in enumerate(NEAR)]


def middle_blocks(chunk):
    out = [(5 + k, chunk, d) for k, d in enumerate(DIAGONAL)]
    return out + [(5 + k, 2, FAR[k]) for k in (chunk, 2 + chunk)]


def last_blocks(chunk):
    return [(9 + k, chunk, d) for k, d in enumerate(KNIGHT)] + [(13 + chunk, None, (2, 2))]


def part_kernel(blocks, first, final, pos, *refs):
    n = len(blocks)
    arrays = sorted({k for k, _, _ in blocks})
    pieces, cols, rest = refs[: len(arrays)], refs[len(arrays) : len(arrays) + 2 * n], refs[len(arrays) + 2 * n :]
    c, sem = rest[-2:]

    @pl.when(pl.program_id(0) == 0)
    def _():
        copies = [
            pltpu.make_async_copy(
                pieces[arrays.index(k)].at[i] if i is not None else pieces[arrays.index(k)],
                c.at[:, :, :, j * COLS : (j + 1) * COLS], sem.at[j]
            )
            for j, (k, i, _) in enumerate(blocks)
        ]
        for x in copies:
            x.start()
        for x in copies:
            x.wait()

    lhs = jnp.concatenate([c[:, 0].reshape(2 * RA, n * COLS), c[:, 1].reshape(2 * RA, n * COLS)], axis=1)
    rhs = jnp.concatenate([x[...] for x in cols], axis=1)
    s = lax.dot_general(lhs, rhs, (((1,), (1,)), ((), ())), preferred_element_type=jnp.float32)
    if not first:
        s += rest[0][...]
    if final:
        split(s.reshape(2, 2, RA // 2, TT), pos[0] == pos[3], pos[4], *rest[-4:-2])
    else:
        rest[-3][...] = s


def part(pos, pieces, train, blocks, acc=None, final=False, tiles=(0, NTL // TT)):
    n = len(blocks)
    arrays = sorted({k for k, _, _ in blocks})
    skip, steps = tiles

    def column(h, d):
        return lambda i, p: (skip + i, h * 16 + lax.rem(p[1] + d[0], 4) * 4 + lax.rem(p[2] + d[1], 4))

    in_specs = [pl.BlockSpec(memory_space=pltpu.HBM)] * len(arrays)
    in_specs += [pl.BlockSpec((TT, COLS), column(h, d)) for h in range(2) for _, _, d in blocks]
    if acc is not None:
        in_specs.append(pl.BlockSpec((2 * RA, TT), lambda i, p: (0, skip + i)))
    if final:
        out_shape = tuple(jax.ShapeDtypeStruct((2, RA // 2, steps * TT), t) for t in (jnp.float32, jnp.bfloat16))
        out_specs = (pl.BlockSpec((2, RA // 2, TT), lambda i, p: (0, 0, i)),) * 2
    else:
        out_shape = jax.ShapeDtypeStruct((2 * RA, NTL), jnp.float32)
        out_specs = pl.BlockSpec((2 * RA, TT), lambda i, p: (0, i))
    return pl.pallas_call(
        functools.partial(part_kernel, blocks, acc is None, final),
        grid_spec=pltpu.PrefetchScalarGridSpec(
            num_scalar_prefetch=1,
            grid=(steps,),
            in_specs=in_specs,
            out_specs=out_specs,
            scratch_shapes=[pltpu.VMEM((2, 2, RA, n * COLS), jnp.bfloat16), pltpu.SemaphoreType.DMA((n,))],
        ),
        out_shape=out_shape,
        compiler_params=pltpu.CompilerParams(vmem_limit_bytes=36 << 20),
        cost_estimate=pl.CostEstimate(
            flops=4 * RA * n * 2 * COLS * steps * TT, bytes_accessed=steps * TT * (n * 512 + RA * 16), transcendentals=0
        ),
        name="part",
    )(pos, *[pieces[k] for k in arrays], *[train] * (2 * n), *([] if acc is None else [acc]))


def score_kernel(chunk, pos, *refs):
    near, two, three, corner, (t, keep, send, c, sem) = refs[:5], refs[5:9], refs[9:13], refs[13:15], refs[15:]
    xh, z, y, xl, core = (pos[i] for i in range(5))

    @pl.when(pl.program_id(0) == 0)
    def _():
        at = lambda d: c.at[:, :, :, pl.ds(pl.multiple_of((((z + d[0]) % 4) * 4 + (y + d[1]) % 4) * COLS, COLS), COLS)]
        copies = [(x.at[chunk], at(d)) for x, d in zip(near, NEAR)]
        copies += [(x.at[chunk], at(d)) for x, d in zip(two, DIAGONAL)]
        copies += [(two[k].at[2], at(FAR[k])) for k in (chunk, 2 + chunk)]
        copies += [(x.at[chunk], at(d)) for x, d in zip(three, KNIGHT)]
        copies += [(corner[chunk], at((2, 2)))]
        copies = [pltpu.make_async_copy(src, dst, sem.at[i]) for i, (src, dst) in enumerate(copies)]
        for x in copies:
            x.start()
        for x in copies:
            x.wait()

    s = 0.0
    for h in range(2):
        s += lax.dot_general(
            c[:, h].reshape(2 * RA, F // 2),
            t[:, h * (F // 2) : (h + 1) * (F // 2)],
            (((1,), (1,)), ((), ())),
            preferred_element_type=jnp.float32,
        )
    split(s.reshape(2, 2, RA // 2, TT), xh == xl, core, keep, send)


def score(pos, pieces, train, chunk, first, steps):
    return pl.pallas_call(
        functools.partial(score_kernel, chunk),
        grid=(steps,),
        out_shape=(
            jax.ShapeDtypeStruct((2, RA // 2, steps * TT), jnp.float32),
            jax.ShapeDtypeStruct((2, RA // 2, steps * TT), jnp.bfloat16),
        ),
        in_specs=[pl.BlockSpec(memory_space=pltpu.SMEM)]
        + [pl.BlockSpec(memory_space=pltpu.HBM)] * 15
        + [pl.BlockSpec((TT, F), lambda i: (i + first, 0))],
        out_specs=(
            pl.BlockSpec((2, RA // 2, TT), lambda i: (0, 0, i)),
            pl.BlockSpec((2, RA // 2, TT), lambda i: (0, 0, i)),
        ),
        scratch_shapes=[pltpu.VMEM((2, 2, RA, F // 2), jnp.bfloat16), pltpu.SemaphoreType.DMA((16,))],
        compiler_params=pltpu.CompilerParams(vmem_limit_bytes=36 << 20),
        cost_estimate=pl.CostEstimate(
            flops=2 * 2 * RA * F * steps * TT, bytes_accessed=(RA * F * 4 + steps * TT * F * 2), transcendentals=0
        ),
        name="score",
    )(pos, *pieces, train)


def per_device(queries, precond, train_grads):
    r, l = lax.axis_index("rows"), lax.axis_index("layers")
    pos = jnp.stack([r // 16, (r // 4) % 4, r % 4, l // 2, l % 2]).astype(jnp.int32)
    q = queries.reshape(2, SUB, F)
    p = precond.reshape(F, COLS)
    train = pltpu.with_memory_space_constraint(train_grads.reshape(NTL, F), pltpu.HBM)
    p_other = lax.ppermute(p, "rows", XH)
    cond = condition(pos, flood(q), p, p_other)

    partner = lax.ppermute(cond, "rows", XH)
    pieces = flood(jnp.stack([cond, partner], axis=1))
    acc = part(pos, pieces, train, near_blocks(0))
    acc = part(pos, pieces, train, middle_blocks(0), acc)
    out = jnp.zeros((8, 2, SUB, NTL), jnp.float32)

    def reduce(out, keep, send, chunk, first):
        got = lax.ppermute(send, "layers", CORE)
        away = (keep[1] + got[1].astype(jnp.float32)).astype(jnp.bfloat16)
        back = lax.ppermute(away, "layers", XL)
        total = keep[0] + got[0].astype(jnp.float32) + back.astype(jnp.float32)
        width = total.shape[1]
        return lax.dynamic_update_slice(out, total.reshape(8, 1, SUB, width), (0, chunk, 0, first * TT)), away, back

    keep, send = part(pos, pieces, train, last_blocks(0), acc, True)
    send, pieces[14] = lax.optimization_barrier((send, pieces[14]))
    out, away, back = reduce(out, keep, send, 0, 0)
    pos1, _ = lax.optimization_barrier((pos, away))
    keep, send = score(pos1, pieces, train, 1, 0, 3)
    send, _ = lax.optimization_barrier((send, back))
    out, away, _ = reduce(out, keep, send, 1, 0)
    pos2, _ = lax.optimization_barrier((pos1, away))
    out, _, _ = reduce(out, *score(pos2, pieces, train, 1, 3, 1), 1, 3)
    return out.reshape(256, NTL)


def solution(mesh):
    return jax.shard_map(
        per_device,
        mesh=mesh,
        in_specs=(P("rows", "layers", None), P("layers", None, "rows"), P("rows", "layers", None)),
        out_specs=P("layers", "rows"),
        check_vma=False,
    )
```

```python
import functools

import jax
import jax.numpy as jnp
from jax import lax
from jax.experimental.layout import Layout, with_layout_constraint
from jax.experimental import pallas as pl
from jax.experimental.pallas import tpu as pltpu
from jax.sharding import PartitionSpec as P

F = 4096
COLS = 128
SUB = 16
RA = 16 * SUB
TT = 512
NTL = 2048


def perm_of(f):
    pairs = []
    for r in range(32):
        xh, z, y = r // 16, (r // 4) % 4, r % 4
        a, b, c = f(xh, z, y)
        pairs.append((r, (a % 2) * 16 + (b % 4) * 4 + c % 4))
    return pairs


UP_Y = perm_of(lambda a, b, c: (a, b, c + 1))
DOWN_Y = perm_of(lambda a, b, c: (a, b, c - 1))
UP_Z = perm_of(lambda a, b, c: (a, b + 1, c))
DOWN_Z = perm_of(lambda a, b, c: (a, b - 1, c))
FAR_Y = perm_of(lambda a, b, c: (a, b, c + 2))
FAR_Z = perm_of(lambda a, b, c: (a, b + 2, c))
XH = perm_of(lambda a, b, c: (a + 1, b, c))
CORE = [(0, 1), (1, 0), (2, 3), (3, 2)]
XL = [(0, 2), (2, 0), (1, 3), (3, 1)]


def send4(to_up_y, to_down_y, to_up_z, to_down_z):
    return [
        lax.ppermute(x, "rows", perm)
        for x, perm in ((to_up_y, UP_Y), (to_down_y, DOWN_Y), (to_up_z, UP_Z), (to_down_z, DOWN_Z))
    ]


NEAR = ((0, 0), (0, 3), (0, 1), (3, 0), (1, 0))
DIAGONAL = ((3, 3), (1, 1), (3, 1), (1, 3))
FAR = ((0, 2), (0, 2), (2, 0), (2, 0))
KNIGHT = ((3, 2), (1, 2), (2, 1), (2, 3))


def flood(block):
    near = [block] + send4(block, block, block, block)
    _, ly, ry, lz, rz = near
    cat = lambda a, b: jnp.concatenate([a, b], axis=0)
    two = send4(cat(lz, ly[:1]), cat(rz, ry[1:]), cat(ry, lz[:1]), cat(ly, rz[1:]))
    corner0 = lax.ppermute(two[2][2], "rows", FAR_Y)
    three = send4(*[x[:2] for x in two])
    corner1 = lax.ppermute(two[1][2], "rows", FAR_Z)
    return [*near, *two, *three, corner0, corner1]


def condition_kernel(pos, *refs):
    near, two, three, corner = refs[:5], refs[5:9], refs[9:13], refs[13:15]
    own, other, out, q, p, sem = refs[15:]
    xh, z, y = pos[0], pos[1], pos[2]
    at = lambda d: ((z + d[0]) % 4) * 4 + (y + d[1]) % 4
    copies = [(own, p.at[:, pl.ds(pl.multiple_of(xh * COLS, COLS), COLS)])]
    copies += [(other, p.at[:, pl.ds(pl.multiple_of((1 - xh) * COLS, COLS), COLS)])]
    copies += [(x, q.at[at(d)]) for x, d in zip(near, NEAR)]
    copies += [(x.at[0:2], q.at[at(d)]) for x, d in zip(two, DIAGONAL)]
    copies += [(x.at[2], q.at[at(d), k % 2]) for k, (x, d) in enumerate(zip(two, FAR))]
    copies += [(x, q.at[at(d)]) for x, d in zip(three, KNIGHT)]
    copies += [(x, q.at[at((2, 2)), k]) for k, x in enumerate(corner)]
    copies = [pltpu.make_async_copy(src, dst, sem.at[i]) for i, (src, dst) in enumerate(copies)]
    for c in copies:
        c.start()
    for c in copies:
        c.wait()
    s = jnp.dot(q[...].reshape(2 * RA, F), p[...], preferred_element_type=jnp.float32)
    s = s.astype(jnp.bfloat16).reshape(16, 2, SUB, 2 * COLS)
    for chunk in range(2):
        for h in range(2):
            out[chunk, h] = s[:, chunk, :, h * COLS : (h + 1) * COLS].reshape(RA, COLS)


def condition(pos, pieces, own, other):
    return pl.pallas_call(
        condition_kernel,
        out_shape=jax.ShapeDtypeStruct((2, 2, RA, COLS), jnp.bfloat16),
        in_specs=[pl.BlockSpec(memory_space=pltpu.SMEM)]
        + [pl.BlockSpec(memory_space=pltpu.HBM)] * 15
        + [pl.BlockSpec(memory_space=pl.ANY)] * 2,
        out_specs=pl.BlockSpec(memory_space=pltpu.VMEM),
        scratch_shapes=[
            pltpu.VMEM((16, 2, SUB, F), jnp.bfloat16),
            pltpu.VMEM((F, 2 * COLS), jnp.bfloat16),
            pltpu.SemaphoreType.DMA((21,)),
        ],
        compiler_params=pltpu.CompilerParams(vmem_limit_bytes=24 << 20),
        cost_estimate=pl.CostEstimate(flops=4 * RA * F * 256, bytes_accessed=6 << 20, transcendentals=0),
        name="condition",
    )(pos, *pieces, own, other)


def split(s, same, core, keep, send):
    for i in range(2):
        own = jnp.where(same, s[i], s[1 - i])
        keep[i] = jnp.where(core == 0, own[0], own[1])
        send[i] = jnp.where(core == 0, own[1], own[0]).astype(jnp.bfloat16)


def near_blocks(chunk):
    return [(k, chunk, d) for k, d in enumerate(NEAR)]


def middle_blocks(chunk):
    out = [(5 + k, chunk, d) for k, d in enumerate(DIAGONAL)]
    return out + [(5 + k, 2, FAR[k]) for k in (chunk, 2 + chunk)]


def last_blocks(chunk):
    return [(9 + k, chunk, d) for k, d in enumerate(KNIGHT)] + [(13 + chunk, None, (2, 2))]


def part_kernel(blocks, first, final, pos, *refs):
    n = len(blocks)
    arrays = sorted({k for k, _, _ in blocks})
    pieces, cols, rest = refs[: len(arrays)], refs[len(arrays) : len(arrays) + 2 * n], refs[len(arrays) + 2 * n :]
    c, sem = rest[-2:]

    @pl.when(pl.program_id(0) == 0)
    def _():
        copies = [
            pltpu.make_async_copy(
                pieces[arrays.index(k)].at[i] if i is not None else pieces[arrays.index(k)],
                c.at[:, :, :, j * COLS : (j + 1) * COLS], sem.at[j]
            )
            for j, (k, i, _) in enumerate(blocks)
        ]
        for x in copies:
            x.start()
        for x in copies:
            x.wait()

    lhs = jnp.concatenate([c[:, 0].reshape(2 * RA, n * COLS), c[:, 1].reshape(2 * RA, n * COLS)], axis=1)
    rhs = jnp.concatenate([x[...] for x in cols], axis=1)
    s = lax.dot_general(lhs, rhs, (((1,), (1,)), ((), ())), preferred_element_type=jnp.float32)
    if not first:
        s += rest[0][...]
    if final:
        split(s.reshape(2, 2, RA // 2, TT), pos[0] == pos[3], pos[4], *rest[-4:-2])
    else:
        rest[-3][...] = s


def part(pos, pieces, train, blocks, acc=None, final=False, tiles=(0, NTL // TT)):
    n = len(blocks)
    arrays = sorted({k for k, _, _ in blocks})
    skip, steps = tiles

    def column(h, d):
        return lambda i, p: (skip + i, h * 16 + lax.rem(p[1] + d[0], 4) * 4 + lax.rem(p[2] + d[1], 4))

    in_specs = [pl.BlockSpec(memory_space=pltpu.HBM)] * len(arrays)
    in_specs += [pl.BlockSpec((TT, COLS), column(h, d)) for h in range(2) for _, _, d in blocks]
    if acc is not None:
        in_specs.append(pl.BlockSpec((2 * RA, TT), lambda i, p: (0, skip + i)))
    if final:
        out_shape = tuple(jax.ShapeDtypeStruct((2, RA // 2, steps * TT), t) for t in (jnp.float32, jnp.bfloat16))
        out_specs = (pl.BlockSpec((2, RA // 2, TT), lambda i, p: (0, 0, i)),) * 2
    else:
        out_shape = jax.ShapeDtypeStruct((2 * RA, NTL), jnp.float32)
        out_specs = pl.BlockSpec((2 * RA, TT), lambda i, p: (0, i))
    return pl.pallas_call(
        functools.partial(part_kernel, blocks, acc is None, final),
        grid_spec=pltpu.PrefetchScalarGridSpec(
            num_scalar_prefetch=1,
            grid=(steps,),
            in_specs=in_specs,
            out_specs=out_specs,
            scratch_shapes=[pltpu.VMEM((2, 2, RA, n * COLS), jnp.bfloat16), pltpu.SemaphoreType.DMA((n,))],
        ),
        out_shape=out_shape,
        compiler_params=pltpu.CompilerParams(vmem_limit_bytes=36 << 20),
        cost_estimate=pl.CostEstimate(
            flops=4 * RA * n * 2 * COLS * steps * TT, bytes_accessed=steps * TT * (n * 512 + RA * 16), transcendentals=0
        ),
        name="part",
    )(pos, *[pieces[k] for k in arrays], *[train] * (2 * n), *([] if acc is None else [acc]))


def score_kernel(chunk, pos, *refs):
    near, two, three, corner, (t, keep, send, c, sem) = refs[:5], refs[5:9], refs[9:13], refs[13:15], refs[15:]
    xh, z, y, xl, core = (pos[i] for i in range(5))

    @pl.when(pl.program_id(0) == 0)
    def _():
        at = lambda d: c.at[:, :, :, pl.ds(pl.multiple_of((((z + d[0]) % 4) * 4 + (y + d[1]) % 4) * COLS, COLS), COLS)]
        copies = [(x.at[chunk], at(d)) for x, d in zip(near, NEAR)]
        copies += [(x.at[chunk], at(d)) for x, d in zip(two, DIAGONAL)]
        copies += [(two[k].at[2], at(FAR[k])) for k in (chunk, 2 + chunk)]
        copies += [(x.at[chunk], at(d)) for x, d in zip(three, KNIGHT)]
        copies += [(corner[chunk], at((2, 2)))]
        copies = [pltpu.make_async_copy(src, dst, sem.at[i]) for i, (src, dst) in enumerate(copies)]
        for x in copies:
            x.start()
        for x in copies:
            x.wait()

    s = 0.0
    for h in range(2):
        s += lax.dot_general(
            c[:, h].reshape(2 * RA, F // 2),
            t[:, h * (F // 2) : (h + 1) * (F // 2)],
            (((1,), (1,)), ((), ())),
            preferred_element_type=jnp.float32,
        )
    split(s.reshape(2, 2, RA // 2, -1), xh == xl, core, keep, send)


def score(pos, pieces, train, chunk, first, steps, TT=TT):
    return pl.pallas_call(
        functools.partial(score_kernel, chunk),
        grid=(steps,),
        out_shape=(
            jax.ShapeDtypeStruct((2, RA // 2, steps * TT), jnp.float32),
            jax.ShapeDtypeStruct((2, RA // 2, steps * TT), jnp.bfloat16),
        ),
        in_specs=[pl.BlockSpec(memory_space=pltpu.SMEM)]
        + [pl.BlockSpec(memory_space=pltpu.HBM)] * 15
        + [pl.BlockSpec((TT, F), lambda i: (i + first, 0))],
        out_specs=(
            pl.BlockSpec((2, RA // 2, TT), lambda i: (0, 0, i)),
            pl.BlockSpec((2, RA // 2, TT), lambda i: (0, 0, i)),
        ),
        scratch_shapes=[pltpu.VMEM((2, 2, RA, F // 2), jnp.bfloat16), pltpu.SemaphoreType.DMA((16,))],
        compiler_params=pltpu.CompilerParams(vmem_limit_bytes=36 << 20),
        cost_estimate=pl.CostEstimate(
            flops=2 * 2 * RA * F * steps * TT, bytes_accessed=(RA * F * 4 + steps * TT * F * 2), transcendentals=0
        ),
        name="score",
    )(pos, *pieces, train)


def per_device(queries, precond, train_grads):
    r, l = lax.axis_index("rows"), lax.axis_index("layers")
    pos = jnp.stack([r // 16, (r // 4) % 4, r % 4, l // 2, l % 2]).astype(jnp.int32)
    q = queries.reshape(2, SUB, F)
    p = precond.reshape(F, COLS)
    train = pltpu.with_memory_space_constraint(train_grads.reshape(NTL, F), pltpu.HBM)
    p_other = lax.ppermute(p, "rows", XH)
    cond = condition(pos, flood(q), p, p_other)

    partner = lax.ppermute(cond, "rows", XH)
    pieces = flood(jnp.stack([cond, partner], axis=1))
    acc = part(pos, pieces, train, near_blocks(0))
    acc = part(pos, pieces, train, middle_blocks(0), acc)
    out = jnp.zeros((8, 2, SUB, NTL), jnp.float32)

    def reduce(out, keep, send, chunk, first):
        got = lax.ppermute(send, "layers", CORE)
        away = (keep[1] + got[1].astype(jnp.float32)).astype(jnp.bfloat16)
        back = lax.ppermute(away, "layers", XL)
        total = keep[0] + got[0].astype(jnp.float32) + back.astype(jnp.float32)
        width = total.shape[1]
        out = lax.dynamic_update_slice(out, total.reshape(8, 1, SUB, width), (0, chunk, 0, first * TT))
        return with_layout_constraint(out, Layout((0, 1, 2, 3))), away, back

    keep, send = part(pos, pieces, train, last_blocks(0), acc, True)
    send, pieces[14] = lax.optimization_barrier((send, pieces[14]))
    out, away, back = reduce(out, keep, send, 0, 0)
    pos1, _ = lax.optimization_barrier((pos, away))
    keep, send = score(pos1, pieces, train, 1, 0, 3)
    send, _ = lax.optimization_barrier((send, back))
    out, away, _ = reduce(out, keep, send, 1, 0)
    pos2, _ = lax.optimization_barrier((pos1, away))
    out, _, _ = reduce(out, *score(pos2, pieces, train, 1, 6, 2, TT // 2), 1, 3)
    return out.reshape(256, NTL)


def solution(mesh):
    return jax.shard_map(
        per_device,
        mesh=mesh,
        in_specs=(P("rows", "layers", None), P("layers", None, "rows"), P("rows", "layers", None)),
        out_specs=P("layers", "rows"),
        check_vma=False,
    )
```
